32 devices in a mesh: row: 8 (over z, core), col: 4 (over y, x).
Axes of the slice: x: 2, y: 2, z: 4, core: 2. Of those that a mesh axis runs over, the one named last changes fastest.
Arguments:
- kkt: float32 [16384, 8, 4, 512], P('row', None, 'col'), as said below
- flow_grad: float32 [16384, 256], P(('row', 'col')), may hold values from -18 to 18
- perm: int32 [16384], P(('row', 'col')), may hold values from 0 to 16383, as said below
Outputs:
- line_grad: float32 [16384, 256], P(('row', 'col'))
- true_residual: float32 [16384, 256], P(('row', 'col'))
The draws below stay inside these ranges and needn't reach their ends.
Inputs may be any that keep to these rules, and one draw needn't show every extreme that they name: Read as a 16384 x 16384 matrix as in the first step, kkt is symmetric and positive definite. perm is a permutation. The 512 lines of each aligned block (lines f * 512 to (f + 1) * 512 - 1) have at most 32 of their KKT rows in any one aligned block of 512 KKT rows, and exactly 32 in some.
All inputs are finite; a program needn't handle non-finite values.
Results may differ from the reference program's by a relative error of at most 0.0003.
Values sent between devices are 32-bit elements; how exact they have to be, the bound alone decides.
No kernel may reach another device: no remote copies, remote signals or barrier semaphores. Data moves between devices by JAX's collectives and lax.ppermute only.
A program may use at most 256 MiB of HBM per device.

```python
import math
import jax
import jax.numpy as jnp
from jax import lax

M = 16384
INTERVALS = 256
ITERS = 2
PIECE = 512
CAP = 32
N_ROW = 8
N_COL = 4


def draw_kkt(key, part):
    key_noise, key_diag = jax.random.split(key)
    spread = 1.98 / math.sqrt(M)
    noise = jax.random.uniform(key_noise, (M, M), jnp.float32, -1.0, 1.0) * (spread * math.sqrt(3.0))
    diagonal = jax.random.uniform(key_diag, (M,), jnp.float32, 4.5, 9.0)
    symmetric = (noise + noise.T) * 0.5
    index = jnp.arange(M)
    matrix = jnp.where(index[:, None] == index[None, :], diagonal[:, None], symmetric)
    return matrix.reshape(M, N_ROW, N_COL, PIECE)


def draw_flow_grad(key, part):
    key_base = jax.random.fold_in(key, 0)
    base = jnp.clip(jax.random.normal(key_base, (M, INTERVALS + 1), jnp.float32), -4.5, 4.5)
    values = 2.0 * (base[:, :-1] + base[:, 1:])
    return values.astype(jnp.float32)


def draw_perm(key, part):
    device_total = N_ROW * N_COL
    key_order, key_source, key_target = jax.random.split(key, 3)
    high_count = PIECE // (2 * CAP)
    middle_count = PIECE // CAP
    ranking = jnp.arange(device_total)
    ranked = jnp.where(ranking < high_count, CAP, jnp.where(ranking < high_count + middle_count, CAP // 2, 0)).astype(jnp.int32)
    offset_order = jax.random.permutation(key_order, device_total)
    per_offset = jnp.zeros((device_total,), jnp.int32).at[offset_order].set(ranked)
    upto = jnp.cumsum(per_offset)
    position = jnp.arange(PIECE)
    offset_of = jnp.sum((upto[None, :] <= position[:, None]).astype(jnp.int32), axis=1)

    def shuffled(subkey):
        scores = jax.random.randint(subkey, (device_total, PIECE), 0, PIECE) * PIECE + position[None, :]
        return jnp.argsort(scores, axis=1).astype(jnp.int32)
    source_order = shuffled(key_source)
    target_order = shuffled(key_target)
    source = ranking[:, None]
    target = (source + offset_of[None, :]) % device_total
    lines = source * PIECE + source_order
    targets = target * PIECE + target_order[target, position[None, :]]
    return jnp.zeros((M,), jnp.int32).at[lines.reshape(-1)].set(targets.reshape(-1).astype(jnp.int32))


def setup_inputs(seed: int = 0) -> dict:
    keys = jax.random.split(jax.random.key(seed), 4)
    kkt = draw_kkt(jax.random.fold_in(keys[3], 71), 0)
    flow_grad = draw_flow_grad(jax.random.fold_in(keys[3], 71), 0)
    perm = draw_perm(jax.random.fold_in(keys[3], 71), 0)
    return {"kkt": kkt, "flow_grad": flow_grad, "perm": perm}


relaxation = 0.15

def solve_definite(matrix, right):
    factor = jnp.linalg.cholesky(matrix)
    return jax.scipy.linalg.cho_solve((factor, True), right)

def reference(kkt, flow_grad, perm):
    highest = lax.Precision.HIGHEST
    matrix = kkt.reshape(M, M)
    rhs = jnp.zeros((M, INTERVALS), jnp.float32).at[perm].set(flow_grad)

    def gram_matrix(left, right):
        return jnp.dot(left.T.astype(jnp.float32), right.astype(jnp.float32), precision=highest, preferred_element_type=jnp.float32)
    solution = jnp.zeros((M, INTERVALS), jnp.float32)
    residual = rhs
    direction = rhs
    norm_gram = gram_matrix(residual, residual)
    for iteration in range(ITERS):
        applied = jnp.dot(matrix.astype(jnp.float32), direction.astype(jnp.float32), precision=highest, preferred_element_type=jnp.float32)
        curvature = gram_matrix(direction, applied)
        step_coef = solve_definite(curvature, norm_gram)
        solution = solution + jnp.dot(direction.astype(jnp.float32), step_coef.astype(jnp.float32), precision=highest, preferred_element_type=jnp.float32)
        residual = residual - jnp.dot(applied.astype(jnp.float32), step_coef.astype(jnp.float32), precision=highest, preferred_element_type=jnp.float32)
        if iteration + 1 < ITERS:
            fresh = gram_matrix(residual, residual)
            mixing = solve_definite(norm_gram, fresh)
            direction = residual + jnp.dot(direction.astype(jnp.float32), mixing.astype(jnp.float32), precision=highest, preferred_element_type=jnp.float32)
            norm_gram = fresh
    refined = solution + relaxation * residual
    true_residual = rhs - jnp.dot(matrix.astype(jnp.float32), refined.astype(jnp.float32), precision=highest, preferred_element_type=jnp.float32)
    line_grad = -refined[perm]
    return (line_grad, true_residual)
```

```python
import functools

import jax
import jax.numpy as jnp
from jax import lax
from jax.experimental import pallas as pl
from jax.experimental.pallas import tpu as pltpu
from jax.sharding import PartitionSpec as P

RELAXATION = 0.15
AXES = ("row", "col")
LANES = 128
PIVOTS = 32


def gram_matrix(left, right):
    return lax.dot_general(
        left,
        right,
        (((0,), (0,)), ((), ())),
        precision=lax.Precision.HIGHEST,
        preferred_element_type=jnp.float32,
    )


def times_small(left, right):
    return jnp.dot(left, right, precision=lax.Precision.HIGHEST, preferred_element_type=jnp.float32)


def invert_small(matrix):
    side = matrix.shape[0]
    down = lax.broadcasted_iota(jnp.int32, (side, side), 0)
    across = lax.broadcasted_iota(jnp.int32, (side, side), 1)
    for k in range(side):
        scale = 1.0 / matrix[k : k + 1, k : k + 1]
        row = jnp.where(across[:1] == k, scale, matrix[k : k + 1, :] * scale)
        rest = jnp.where(across == k, 0.0, matrix) - matrix[:, k : k + 1] * row
        matrix = jnp.where(down == k, row, rest)
    return matrix


def inverse_kernel(matrix_ref, out_ref):
    side = matrix_ref.shape[0]
    out_ref[...] = matrix_ref[...]
    for start in range(0, side, PIVOTS):
        here = slice(start, start + PIVOTS)
        pivot = invert_small(out_ref[here, here])
        rows = times_small(pivot, out_ref[here, :])
        columns = out_ref[:, here]
        update = times_small(columns, rows)
        corner = times_small(columns, pivot)
        out_ref[...] = out_ref[...] - update
        out_ref[:, here] = -corner
        out_ref[here, :] = rows
        out_ref[here, here] = pivot


def inverse_definite(matrix):
    return pl.pallas_call(
        inverse_kernel,
        out_shape=jax.ShapeDtypeStruct(matrix.shape, jnp.float32),
        name="inverse_definite",
    )(matrix)


def solve_refined(inverse, matrix, right):
    answer = times_small(inverse, right)
    return answer + times_small(inverse, right - times_small(matrix, answer))


def exchange(blocks):
    return lax.all_to_all(blocks, AXES, split_axis=0, concat_axis=0, tiled=True)


def sum_everywhere(stacked, device_count):
    rows, width = stacked.shape
    slab = exchange(stacked.reshape(device_count, rows // device_count, width)).sum(axis=0)
    return exchange(jnp.broadcast_to(slab[None], (device_count,) + slab.shape)).reshape(rows, width)


def split_kernel(where_ref, tile_ref, high_ref, low_ref, *, side):
    block = high_ref.shape[0]
    chunks = high_ref.shape[1] // LANES
    first_row, first_column = where_ref[0], where_ref[1]
    down = lax.broadcasted_iota(jnp.int32, (block, LANES), 0) + pl.program_id(0) * block - first_row
    across = lax.broadcasted_iota(jnp.int32, (block, LANES), 1) - first_column
    gap = jnp.where((down >= 0) & (down < side), across - down, LANES * chunks * 4)
    for chunk in range(chunks):
        piece = tile_ref[pl.ds(chunk, block, stride=chunks), :]
        piece = jnp.where(gap == -chunk * LANES, 0.0, piece)
        high = piece.astype(jnp.bfloat16)
        low = (piece - high.astype(jnp.float32)).astype(jnp.bfloat16)
        high_ref[:, chunk * LANES : (chunk + 1) * LANES] = high
        low_ref[:, chunk * LANES : (chunk + 1) * LANES] = low


def split_matrix(kkt, where, side):
    rows = kkt.shape[0]
    width = kkt.shape[1] * kkt.shape[2] * kkt.shape[3]
    chunks = width // LANES
    block = min(128, rows)
    out = jax.ShapeDtypeStruct((rows, width), jnp.bfloat16)
    return pl.pallas_call(
        functools.partial(split_kernel, side=side),
        grid=(rows // block,),
        in_specs=[
            pl.BlockSpec(memory_space=pltpu.SMEM),
            pl.BlockSpec((block * chunks, LANES), lambda i: (i, 0)),
        ],
        out_specs=[pl.BlockSpec((block, width), lambda i: (i, 0))] * 2,
        out_shape=[out, out],
        name="split_matrix",
    )(where, kkt.reshape(rows * chunks, LANES))


def product_kernel(high_ref, low_ref, vector_ref, out_ref, vector_high, vector_low):
    @pl.when(pl.program_id(0) == 0)
    def _():
        vector = vector_ref[...]
        high = vector.astype(jnp.bfloat16)
        vector_high[...] = high
        vector_low[...] = (vector - high.astype(jnp.float32)).astype(jnp.bfloat16)

    def dot(left, right):
        return jnp.dot(left, right, preferred_element_type=jnp.float32)

    high = high_ref[...]
    small = dot(high, vector_low[...]) + dot(low_ref[...], vector_high[...])
    out_ref[...] = small + dot(high, vector_high[...])


def tile_product(high, low, vector):
    rows, width = high.shape
    count = vector.shape[1]
    block = min(256, rows)
    return pl.pallas_call(
        product_kernel,
        grid=(rows // block,),
        in_specs=[
            pl.BlockSpec((block, width), lambda i: (i, 0)),
            pl.BlockSpec((block, width), lambda i: (i, 0)),
            pl.BlockSpec((width, count), lambda i: (0, 0)),
        ],
        out_specs=pl.BlockSpec((block, count), lambda i: (i, 0)),
        out_shape=jax.ShapeDtypeStruct((rows, count), jnp.float32),
        scratch_shapes=[pltpu.VMEM((width, count), jnp.bfloat16)] * 2,
        name="tile_product",
    )(high, low, vector)


def on_device(kkt, flow_grad, perm):
    highest = lax.Precision.HIGHEST
    device_count = lax.axis_size("row") * lax.axis_size("col")
    block_rows, interval_count = flow_grad.shape
    capacity = 2 * max(1, block_rows // device_count)
    slot_total = device_count * capacity
    owner = perm // block_rows
    local_row = perm % block_rows
    position = jnp.arange(block_rows)
    earlier = (owner[None, :] == owner[:, None]) & (position[None, :] < position[:, None])
    slot_index = jnp.sum(earlier.astype(jnp.int32), axis=1)
    slot_key = owner * capacity + slot_index
    onehot = jnp.arange(slot_total)[:, None] == slot_key[None, :]
    selector = onehot.astype(jnp.float32)
    send_rows = jnp.dot(selector, flow_grad, precision=highest, preferred_element_type=jnp.float32)
    send_index = jnp.sum(jnp.where(onehot, local_row[None, :] + 1, 0), axis=1) - 1
    row_place, col_place = lax.axis_index("row"), lax.axis_index("col")
    where = jnp.stack([col_place, row_place]).astype(jnp.int32) * block_rows
    slab = lax.dynamic_slice(
        kkt, (col_place * block_rows, row_place, 0, 0), (block_rows, 1, 1, block_rows)
    ).reshape(block_rows, block_rows)
    diagonal = jnp.sum(jnp.where(position[:, None] == position[None, :], slab, 0.0), axis=1)[:, None]
    places = jnp.pad(
        send_index.astype(jnp.float32).reshape(device_count, 1, capacity),
        ((0, 0), (0, 0), (0, interval_count - capacity)),
    )
    lane = lax.broadcasted_iota(jnp.int32, places.shape, 2)
    places = jnp.where(lane == capacity, jnp.sum(diagonal), places)
    arrived = exchange(
        jnp.concatenate(
            [send_rows.reshape(device_count, capacity, interval_count), places], axis=1
        )
    )
    received = arrived[:, :capacity]
    received_index = arrived[:, capacity, :capacity].astype(jnp.int32)
    high, low = split_matrix(kkt, where, block_rows)
    shift = jnp.sum(arrived[:, capacity, capacity]) / (device_count * block_rows)
    shifted_diagonal = diagonal - shift
    landing = (position[:, None] == received_index.reshape(slot_total)[None, :]).astype(jnp.float32)
    rhs = jnp.dot(
        landing,
        received.reshape(slot_total, interval_count),
        precision=highest,
        preferred_element_type=jnp.float32,
    )

    def gather(vector):
        return lax.all_gather(vector, "row", axis=0, tiled=True)

    def apply_operator(vector, gathered):
        partial_rows = tile_product(high, low, gathered)
        summed = lax.psum_scatter(partial_rows, "col", scatter_dimension=0, tiled=True)
        return summed + shifted_diagonal * vector

    norm_gram = sum_everywhere(gram_matrix(flow_grad, flow_grad), device_count)

    first = apply_operator(rhs, gather(rhs))
    first, norm_gram = lax.optimization_barrier((first, norm_gram))

    first_gathered = gather(first)
    norm_inverse = inverse_definite(norm_gram)
    sums = sum_everywhere(
        jnp.concatenate([gram_matrix(rhs, first), gram_matrix(first, first)], axis=0), device_count
    )
    first_gathered, sums, norm_inverse = lax.optimization_barrier((first_gathered, sums, norm_inverse))
    second = apply_operator(first, first_gathered)
    cross_gram, image_gram = jnp.split(sums, 2, axis=0)
    identity = jnp.eye(interval_count, dtype=jnp.float32)
    curvature = cross_gram + shift * norm_gram
    step_coef = solve_refined(inverse_definite(curvature), curvature, norm_gram)
    keep = identity - shift * step_coef
    cross = gram_matrix(keep, times_small(cross_gram, step_coef))
    fresh = (
        gram_matrix(keep, times_small(norm_gram, keep))
        - cross
        - cross.T
        + gram_matrix(step_coef, times_small(image_gram, step_coef))
    )
    mixing = keep + solve_refined(norm_inverse, norm_gram, fresh)
    second, mixing, step_coef = lax.optimization_barrier((second, mixing, step_coef))

    second_gathered = gather(second)
    direction = times_small(rhs, mixing) - times_small(first, step_coef)
    applied = shift * direction + times_small(first, mixing) - times_small(second, step_coef)
    curvature = sum_everywhere(gram_matrix(direction, applied), device_count)
    next_coef = solve_refined(inverse_definite(curvature), curvature, fresh)

    moved = times_small(mixing, next_coef)
    both = times_small(step_coef, next_coef)
    on_rhs = step_coef + moved + RELAXATION * (keep - shift * moved)
    on_first = -both - RELAXATION * (step_coef + moved - shift * both)
    on_second = RELAXATION * both
    refined = times_small(rhs, on_rhs) + times_small(first, on_first) + times_small(second, on_second)
    so_far = (
        times_small(rhs, identity - shift * on_rhs)
        - times_small(first, on_rhs + shift * on_first)
        - times_small(second, on_first + shift * on_second)
    )
    back_rows = gram_matrix(landing, refined)
    second_gathered, back_rows = lax.optimization_barrier((second_gathered, back_rows))
    third = apply_operator(second, second_gathered)
    returned = exchange(back_rows.reshape(device_count, capacity, interval_count))
    line_grad = -gram_matrix(selector, returned.reshape(slot_total, interval_count))
    true_residual = so_far - times_small(third, on_second)
    return (line_grad, true_residual)


def solution(mesh):
    in_specs = (P("row", None, "col", None), P(AXES, None), P(AXES))
    out_specs = (P(AXES, None), P(AXES, None))
    return jax.shard_map(
        on_device, mesh=mesh, in_specs=in_specs, out_specs=out_specs, check_vma=False
    )
```
